32 devices in a mesh: dp: 8 (over z, x), tensor: 4 (over y, core).
Axes of the slice: x: 2, y: 2, z: 4, core: 2. Of those that a mesh axis runs over, the one named last changes fastest.
Arguments:
- tokens: bfloat16 [16384, 1024], P(('dp', 'tensor')), may hold values from -6 to 6
- cotangent: bfloat16 [16384, 1024], P(('dp', 'tensor')), may hold values from -6 to 6
- lengths: int32 [8, 16], P('dp'), may hold values from 1 to 256, 2048 in all within a row
- qkv_master: float32 [1024, 3, 1024], P('dp', None, 'tensor'), may hold values from -0.1875 to 0.1875
- qkv_first: float32 [1024, 3, 1024], P('dp', None, 'tensor'), may hold values from -0.00015258789 to 0.00015258789
- qkv_second: float32 [1024, 3, 1024], P('dp', None, 'tensor'), may hold values from 2.9798684e-11 to 4.7677895e-10
- out_master: float32 [1024, 1024], P(('tensor', 'dp')), may hold values from -1 to 1
- out_first: float32 [1024, 1024], P(('tensor', 'dp')), may hold values from -9.1552734e-05 to 9.1552734e-05
- out_second: float32 [1024, 1024], P(('tensor', 'dp')), may hold values from 5.959737e-12 to 9.535579e-11
- in_master: float32 [1024, 2, 4096], P('dp', None, 'tensor'), may hold values from -0.1875 to 0.1875
- in_first: float32 [1024, 2, 4096], P('dp', None, 'tensor'), may hold values from -0.00015258789 to 0.00015258789
- in_second: float32 [1024, 2, 4096], P('dp', None, 'tensor'), may hold values from 2.9798684e-11 to 4.7677895e-10
- down_master: float32 [4096, 1024], P(('tensor', 'dp')), may hold values from -0.09375 to 0.09375
- down_first: float32 [4096, 1024], P(('tensor', 'dp')), may hold values from -0.00015258789 to 0.00015258789
- down_second: float32 [4096, 1024], P(('tensor', 'dp')), may hold values from 2.9798684e-11 to 4.7677895e-10
- norm_gains: float32 [2, 1024], replicated, may hold values from 0.2 to 2.8
- gain_first: float32 [2, 1024], replicated, may hold values from -0.00061035156 to 0.00061035156
- gain_second: float32 [2, 1024], replicated, may hold values from 4.7677895e-10 to 7.628463e-09
Outputs:
- layer_out: bfloat16 [16384, 1024], P(('dp', 'tensor'))
- input_grad: float32 [16384, 1024], P(('dp', 'tensor'))
- qkv_grad: float32 [1024, 3, 1024], P('dp', None, 'tensor')
- qkv_new: float32 [1024, 3, 1024], P('dp', None, 'tensor')
- qkv_first_new: float32 [1024, 3, 1024], P('dp', None, 'tensor')
- qkv_second_new: float32 [1024, 3, 1024], P('dp', None, 'tensor')
- out_grad: float32 [1024, 1024], P(('tensor', 'dp'))
- out_new: float32 [1024, 1024], P(('tensor', 'dp'))
- out_first_new: float32 [1024, 1024], P(('tensor', 'dp'))
- out_second_new: float32 [1024, 1024], P(('tensor', 'dp'))
- in_grad: float32 [1024, 2, 4096], P('dp', None, 'tensor')
- in_new: float32 [1024, 2, 4096], P('dp', None, 'tensor')
- in_first_new: float32 [1024, 2, 4096], P('dp', None, 'tensor')
- in_second_new: float32 [1024, 2, 4096], P('dp', None, 'tensor')
- down_grad: float32 [4096, 1024], P(('tensor', 'dp'))
- down_new: float32 [4096, 1024], P(('tensor', 'dp'))
- down_first_new: float32 [4096, 1024], P(('tensor', 'dp'))
- down_second_new: float32 [4096, 1024], P(('tensor', 'dp'))
- gain_grad: float32 [2, 1024], replicated
- gain_new: float32 [2, 1024], replicated
- gain_first_new: float32 [2, 1024], replicated
- gain_second_new: float32 [2, 1024], replicated
- grad_norm: float32 [], replicated
The draws below stay inside these ranges and needn't reach their ends.
Inputs may be any that keep to these rules, and one draw needn't show every extreme that they name: Each row's 16 window lengths are positive, add up to 2048, and the longest is 256.
All inputs are finite; a program needn't handle non-finite values.
Results may differ from the reference program's by a relative error of at most 0.024.
Values may be sent and summed in bfloat16 or wider, within the bound.
No kernel may reach another device: no remote copies, remote signals or barrier semaphores. Data moves between devices by JAX's collectives and lax.ppermute only.
A program may use at most 192 MiB of HBM per device.

```python
import math
import jax
import jax.numpy as jnp
import numpy as np
from jax import lax

D = 1024
HEADS = 16
HEAD_DIM = 64
FF = 4096
ROW = 2048
SEGS = 16
MOST = 256
STEP = 5
ROWS = 8
TOKENS = 16384


def draw_norm_gains(key, part):
    fraction = jnp.arange(D, dtype=jnp.float32) / D
    rising = 0.5 + fraction
    jitter = 1.0 + 0.3 * jax.random.uniform(key, (2, D), jnp.float32, -1.0, 1.0)
    return rising[None, :] * jitter


def levels(key, extent, split, smallest, top_value):
    level = 1.0
    for axis_at, blocks in split:
        steps = jax.random.uniform(jax.random.fold_in(jax.random.fold_in(key, 6), axis_at), (blocks,), jnp.float32, smallest / len(split), top_value / len(split))
        level = level * jnp.repeat(jnp.exp(steps), extent[axis_at] // blocks).reshape((-1,) + (1,) * (len(extent) - 1 - axis_at))
    return level


def profile(number_of, total, bound, slope):
    weights = [(1 << 20) // math.isqrt(rank ** slope) + 1 for rank in range(2, number_of + 1)]
    surplus, given = total - bound - (number_of - 1), [1] * (number_of - 1)
    while surplus > 0:
        candidates = [i for i in range(number_of - 1) if given[i] < bound]
        mass, left = sum([weights[i] for i in candidates]), surplus
        for i in candidates:
            extra = min(bound - given[i], max(1, left * weights[i] // mass), surplus)
            given[i] = given[i] + extra
            surplus = surplus - extra
    return np.array([bound] + given)


def ragged_sizes(own_key, amount, total, most, skew):
    if amount == 2:
        one = jax.random.randint(own_key, (), max(1, total - most), min(most, total - 1) + 1)
        return jnp.stack([one, total - one])
    tallies = jnp.asarray(profile(amount, total, most, skew), jnp.int32)
    couples = (amount - 1) // 2
    donor, taker = tallies[1:1 + 2 * couples:2], tallies[2:2 + 2 * couples:2]
    room = jnp.minimum(donor - 1, most - taker)
    shifted = jax.random.randint(jax.random.fold_in(own_key, 1), (couples,), 0, 1 << 20) % (room + 1)
    tallies = tallies.at[1:1 + 2 * couples:2].set(donor - shifted).at[2:2 + 2 * couples:2].set(taker + shifted)
    return tallies[jax.random.permutation(jax.random.fold_in(own_key, 2), amount)]


def centred(rng, shape, deviation, bound, shards=(), held_as=jnp.bfloat16):
    level = levels(rng, shape, shards, -0.22, 0.18) if shards else 1.0
    drawn = jax.random.normal(rng, shape, jnp.float32) * deviation * level
    return jnp.minimum(jnp.maximum(drawn, -bound), bound).astype(held_as)


def setup_inputs(seed: int = 0) -> dict:
    seeds = jax.random.split(jax.random.key(seed), 19)
    tokens = centred(seeds[0], (TOKENS, D), 1.0, 6.0, ((0, 32),))
    cotangent = centred(seeds[1], (TOKENS, D), 1.0, 6.0, ((0, 32),))
    lengths = jax.vmap(lambda own: ragged_sizes(own, SEGS, ROW, MOST, 2))(jax.random.split(seeds[2], ROWS)).reshape((ROWS, SEGS)).astype(jnp.int32)
    qkv_master = centred(seeds[3], (D, 3, D), D ** -0.5, 0.1875, ((0, 8), (2, 4)), jnp.float32)
    qkv_first = centred(seeds[4], (D, 3, D), (0.11 / (4 * D * D + 3 * D * FF + 2 * D) ** 0.5), 0.00015258789, ((0, 8), (2, 4)), jnp.float32)
    qkv_second = jnp.clip(jnp.exp(math.log(4.767789496540331e-10) - 2.7725887 * jax.random.uniform(seeds[5], (D, 3, D), jnp.float32) ** levels(seeds[5], (D, 3, D), ((0, 8), (2, 4)), -0.2, 0.2)), 2.979868435337707e-11, 4.767789496540331e-10)
    out_master = centred(seeds[6], (D, D), (D * SEGS * 4 // ROW) ** -0.5, 1.0, ((0, 32),), jnp.float32)
    out_first = centred(seeds[7], (D, D), (0.06 / (4 * D * D + 3 * D * FF + 2 * D) ** 0.5), 9.1552734375e-05, ((0, 32),), jnp.float32)
    out_second = jnp.clip(jnp.exp(math.log(9.535579270636418e-11) - 2.7725887 * jax.random.uniform(seeds[8], (D, D), jnp.float32) ** levels(seeds[8], (D, D), ((0, 32),), -0.2, 0.2)), 5.9597370441477615e-12, 9.535579270636418e-11)
    in_master = centred(seeds[9], (D, 2, FF), D ** -0.5, 0.1875, ((0, 8), (2, 4)), jnp.float32)
    in_first = centred(seeds[10], (D, 2, FF), (0.11 / (4 * D * D + 3 * D * FF + 2 * D) ** 0.5), 0.00015258789, ((0, 8), (2, 4)), jnp.float32)
    in_second = jnp.clip(jnp.exp(math.log(4.767789496540331e-10) - 2.7725887 * jax.random.uniform(seeds[11], (D, 2, FF), jnp.float32) ** levels(seeds[11], (D, 2, FF), ((0, 8), (2, 4)), -0.2, 0.2)), 2.979868435337707e-11, 4.767789496540331e-10)
    down_master = centred(seeds[12], (FF, D), FF ** -0.5, 0.09375, ((0, 32),), jnp.float32)
    down_first = centred(seeds[13], (FF, D), (0.11 / (4 * D * D + 3 * D * FF + 2 * D) ** 0.5), 0.00015258789, ((0, 32),), jnp.float32)
    down_second = jnp.clip(jnp.exp(math.log(4.767789496540331e-10) - 2.7725887 * jax.random.uniform(seeds[14], (FF, D), jnp.float32) ** levels(seeds[14], (FF, D), ((0, 32),), -0.2, 0.2)), 2.979868435337707e-11, 4.767789496540331e-10)
    norm_gains = draw_norm_gains(jax.random.fold_in(seeds[18], 71), 0)
    gain_first = centred(seeds[16], (2, D), (0.44 / (4 * D * D + 3 * D * FF + 2 * D) ** 0.5), 0.00061035156, (), jnp.float32)
    gain_second = jnp.clip(jnp.exp(jax.random.uniform(seeds[17], (2, D), jnp.float32, math.log(4.767789496540331e-10), math.log(7.62846319446453e-09))), 4.767789496540331e-10, 7.62846319446453e-09)
    return dict(tokens=tokens, cotangent=cotangent, lengths=lengths, qkv_master=qkv_master, qkv_first=qkv_first, qkv_second=qkv_second, out_master=out_master, out_first=out_first, out_second=out_second, in_master=in_master, in_first=in_first, in_second=in_second, down_master=down_master, down_first=down_first, down_second=down_second, norm_gains=norm_gains, gain_first=gain_first, gain_second=gain_second)


@jax.custom_vjp
def low(v):
    return lax.optimization_barrier(v.astype(jnp.bfloat16)).astype(jnp.float32)

@jax.custom_vjp
def low_back(v):
    return v

def low_keep(v):
    return (low(v), None)

def low_pass(kept, grad):
    return (grad,)

def back_keep(v):
    return (v, None)

def back_low(kept, grad):
    return (low(grad),)
low.defvjp(low_keep, low_pass)
low_back.defvjp(back_keep, back_low)
highest = lax.Precision.HIGHEST
eps_norm = 1e-05
beta_one = 0.9
beta_two = 0.999
learn_rate = 0.05
gain_rate = 0.6
weight_decay = 0.1
adam_eps = 1e-08
max_norm = 1.0

def layer_norm(values, gain):
    centre = values - lax.optimization_barrier(jnp.mean(values, axis=-1, keepdims=True))
    spread = lax.optimization_barrier(jnp.mean(centre * centre, axis=-1, keepdims=True))
    return centre * lax.rsqrt(spread + eps_norm) * gain

def row_layout(lengths):
    seg_ends = jnp.cumsum(lengths, axis=-1).astype(jnp.int32)
    places = jnp.arange(ROW, dtype=jnp.int32)
    passed = (places[:, None] >= seg_ends[..., None, :]).astype(jnp.int32)
    segment = lax.optimization_barrier(jnp.sum(passed, axis=-1)).astype(jnp.int32)
    offset = places - lax.optimization_barrier(jnp.sum(passed * lengths[..., None, :], axis=-1)).astype(jnp.int32)
    return (segment, offset)

def rotary_tables(offset):
    half_dim = HEAD_DIM // 2
    inverse = jnp.exp(jnp.arange(half_dim, dtype=jnp.float32) * (-2.0 * math.log(10000.0) / HEAD_DIM))
    angles = offset.astype(jnp.float32)[..., None] * inverse
    return (jnp.cos(angles), jnp.sin(angles))

def rotate(values, cosine, sine):
    half_dim = values.shape[-1] // 2
    front_half = values[..., :half_dim]
    back_half = values[..., half_dim:]
    cos_wide = cosine[..., None, :]
    sin_wide = sine[..., None, :]
    return jnp.concatenate([front_half * cos_wide - back_half * sin_wide, back_half * cos_wide + front_half * sin_wide], axis=-1)

def adam_update(weight, first_moment, second_moment, gradient, factor, use_decay, rate):
    clipped = gradient * factor
    first_new = beta_one * first_moment + (1.0 - beta_one) * clipped
    second_new = beta_two * second_moment + (1.0 - beta_two) * clipped * clipped
    first_hat = first_new / (1.0 - beta_one ** STEP)
    second_hat = second_new / (1.0 - beta_two ** STEP)
    direction = first_hat / (jnp.sqrt(second_hat) + adam_eps) + use_decay * weight_decay * weight
    return (clipped, weight - rate * direction, first_new, second_new)

def row_forward(row_x, qkv_w, out_w, in_w, down_w, gain_w, segment, cosine, sine):
    score_scale = HEAD_DIM ** (-0.5)
    block_rows = min(512, ROW)
    block_count = ROW // block_rows
    normed = low(layer_norm(row_x, gain_w[0]))
    projected = low_back(jnp.dot(normed, low(qkv_w).reshape(D, 3 * D), precision=highest))
    projected = projected.reshape(ROW, 3, HEADS, HEAD_DIM)
    queries = low(rotate(projected[:, 0], cosine, sine))
    keys = low(rotate(projected[:, 1], cosine, sine))
    values = low(projected[:, 2])

    def attend(pieces):
        query_block, segment_block = pieces
        scores = low_back(jnp.einsum('qhd,khd->hqk', query_block, keys, precision=highest) * score_scale)
        allowed = segment_block[:, None] == segment[None, :]
        masked = jnp.where(allowed[None], scores, -1e+30)
        row_max = lax.optimization_barrier(jnp.max(masked, axis=-1, keepdims=True))
        log_total = jnp.log(lax.optimization_barrier(jnp.sum(jnp.exp(masked - row_max), axis=-1, keepdims=True))) + row_max
        weights = jnp.exp(masked - log_total)
        return jnp.einsum('hqk,khd->qhd', low(weights), values, precision=highest)
    mixed_heads = lax.map(jax.checkpoint(attend), (queries.reshape(block_count, block_rows, HEADS, HEAD_DIM), segment.reshape(block_count, block_rows)))
    attended = low(low_back(mixed_heads.reshape(ROW, D)))
    branch = low_back(jnp.dot(attended, low(out_w), precision=highest))
    middle = row_x + branch
    normed_two = low(layer_norm(middle, gain_w[1]))
    gate_up = low_back(jnp.dot(normed_two, low(in_w).reshape(D, 2 * FF), precision=highest))
    hidden = low(jax.nn.silu(gate_up[:, :FF]) * gate_up[:, FF:])
    return middle + low_back(jnp.dot(hidden, low(down_w), precision=highest))

def reference(tokens, cotangent, lengths, qkv_master, qkv_first, qkv_second, out_master, out_first, out_second, in_master, in_first, in_second, down_master, down_first, down_second, norm_gains, gain_first, gain_second):
    rows_x = tokens.astype(jnp.float32).reshape(ROWS, ROW, D)
    rows_dy = cotangent.astype(jnp.float32).reshape(ROWS, ROW, D)
    masters = (qkv_master, out_master, in_master, down_master, norm_gains)

    def per_row(totals, pieces):
        row_x, row_dy, row_lengths = pieces
        segment, offset = row_layout(row_lengths)
        cosine, sine = rotary_tables(offset)

        def forward(inputs, qkv_w, out_w, in_w, down_w, gain_w):
            return row_forward(inputs, qkv_w, out_w, in_w, down_w, gain_w, segment, cosine, sine)
        output, pullback = jax.vjp(forward, row_x, qkv_master, out_master, in_master, down_master, norm_gains)
        row_grads = pullback(row_dy)
        totals = jax.tree.map(jnp.add, totals, tuple(row_grads[1:]))
        return (totals, (output, row_grads[0]))
    zeros_init = jax.tree.map(jnp.zeros_like, masters)
    totals, (outputs, input_grads) = lax.scan(per_row, zeros_init, (rows_x, rows_dy, lengths))
    squares = sum((jnp.sum(gradient * gradient) for gradient in totals))
    grad_norm = jnp.sqrt(squares)
    factor = max_norm / jnp.maximum(grad_norm, max_norm)
    qkv_res = adam_update(qkv_master, qkv_first, qkv_second, totals[0], factor, 1.0, learn_rate)
    out_res = adam_update(out_master, out_first, out_second, totals[1], factor, 1.0, learn_rate)
    in_res = adam_update(in_master, in_first, in_second, totals[2], factor, 1.0, learn_rate)
    down_res = adam_update(down_master, down_first, down_second, totals[3], factor, 1.0, learn_rate)
    gain_res = adam_update(norm_gains, gain_first, gain_second, totals[4], factor, 0.0, gain_rate)
    return (outputs.reshape(TOKENS, D).astype(jnp.bfloat16), input_grads.reshape(TOKENS, D), qkv_res[0], qkv_res[1], qkv_res[2], qkv_res[3], out_res[0], out_res[1], out_res[2], out_res[3], in_res[0], in_res[1], in_res[2], in_res[3], down_res[0], down_res[1], down_res[2], down_res[3], gain_res[0], gain_res[1], gain_res[2], gain_res[3], grad_norm)
```

```python
import functools
import math

import jax
import jax.numpy as jnp
from jax import lax
from jax.experimental import pallas as pl
from jax.experimental.pallas import tpu as pltpu
from jax.sharding import PartitionSpec as P

D = 1024
HEADS = 16
HEAD_DIM = 64
FF = 4096
ROW = 2048
STEP = 5
MOST = 256

eps_norm = 1e-05
beta_one = 0.9
beta_two = 0.999
learn_rate = 0.05
gain_rate = 0.6
weight_decay = 0.1
adam_eps = 1e-08
max_norm = 1.0

BF = jnp.bfloat16
F32 = jnp.float32
TP = 4
PIECE = ROW // TP
BLK = 256
SPAN = 3 * BLK
NB = ROW // BLK
HL = HEADS // TP
WL = HL * HEAD_DIM
FL = FF // TP
VMEM_LIMIT = 60 * 1024 * 1024

NT = (((1,), (1,)), ((), ()))
TN = (((0,), (0,)), ((), ()))
NN = (((1,), (0,)), ((), ()))


def mm(a, b, dims=NN):
    return lax.dot_general(a, b, dims, preferred_element_type=F32)


def layer_norm(values, gain):
    centre = values - jnp.mean(values, axis=-1, keepdims=True)
    spread = jnp.mean(centre * centre, axis=-1, keepdims=True)
    return centre * lax.rsqrt(spread + eps_norm) * gain


def swap(x, axis, k):
    return lax.ppermute(x, axis, [(i, i ^ k) for i in range(lax.axis_size(axis))])


def gather_pieces(own):
    near = swap(own, "tensor", 1)
    far = swap(own, "tensor", 2)
    return own, near, far, swap(far, "tensor", 1)


def scatter_sum(p0, p1, p2, p3):
    far = (p2.astype(F32) + swap(p3, "tensor", 1).astype(F32)).astype(BF)
    near = swap(p1, "tensor", 1)
    return p0.astype(F32) + near.astype(F32) + swap(far, "tensor", 2).astype(F32)


def rope_slab(u, cos, sin, lane_low):
    swapped = jnp.where(lane_low, pltpu.roll(u, 128 - 32, 1), pltpu.roll(u, 32, 1))
    return u * cos + swapped * sin


def head_mask(h, rows, dtype):
    lane = lax.broadcasted_iota(jnp.int32, (rows, WL), 1)
    return (lane // HEAD_DIM == h).astype(dtype)


def span_start(i):
    return pl.multiple_of(jnp.clip(i - 1, 0, NB - 3) * BLK, BLK)


def attn_fwd_body(t_ref, a0, a1, a2, a3, w_ref, wo_ref, cos_ref, sin_ref, segc_ref, segr_ref,
                  qkv_ref, o_ref, lse_ref, r0, r1, r2, r3):
    t = t_ref[0]
    low = lax.broadcasted_iota(jnp.int32, (BLK, 128), 1) % HEAD_DIM < HEAD_DIM // 2
    per = PIECE // BLK
    for j, a_ref in enumerate((a0, a1, a2, a3)):
        for half in range(per):
            row = pl.multiple_of((t ^ j) * PIECE + half * BLK, BLK)
            p = mm(a_ref[half * BLK:(half + 1) * BLK, :], w_ref[...])
            cos = cos_ref[pl.ds(row, BLK), :]
            sin = sin_ref[pl.ds(row, BLK), :]
            for s in range(2 * WL // 128):
                u = rope_slab(p[:, s * 128:(s + 1) * 128], cos, sin, low)
                if s < WL // 128:
                    u = u * (HEAD_DIM ** -0.5)
                qkv_ref[pl.ds(row, BLK), s * 128:(s + 1) * 128] = u.astype(BF)
            qkv_ref[pl.ds(row, BLK), 2 * WL:] = p[:, 2 * WL:].astype(BF)
    masks = [head_mask(h, BLK, BF) for h in range(HL)]
    masks_f = [head_mask(h, BLK, F32) for h in range(HL)]
    lane = lax.broadcasted_iota(jnp.int32, (BLK, 128), 1)

    def block(i, carry):
        row = pl.multiple_of(i * BLK, BLK)
        start = span_start(i)
        q = qkv_ref[pl.ds(row, BLK), :WL]
        k = qkv_ref[pl.ds(start, SPAN), WL:2 * WL]
        v = qkv_ref[pl.ds(start, SPAN), 2 * WL:]
        bias = jnp.where(segc_ref[pl.ds(row, BLK), :] == segr_ref[0:1, pl.ds(start, SPAN)], 0.0, -1e30)
        out = jnp.zeros((BLK, WL), F32)
        lse = jnp.zeros((BLK, 128), F32)
        for h in range(HL):
            s = mm(q * masks[h], k, NT) + bias
            top = jnp.max(s, axis=1, keepdims=True)
            e = jnp.exp(s - top)
            total = jnp.sum(e, axis=1, keepdims=True)
            out += mm(e.astype(BF), v) * (1.0 / total) * masks_f[h]
            lse += jnp.where(lane == h, jnp.log(total) + top, 0.0)
        o = out.astype(BF)
        o_ref[pl.ds(row, BLK), :] = o
        lse_ref[:, pl.ds(row, BLK)] = lse.T[:8, :]
        part = mm(o, wo_ref[...]).astype(BF)
        place = pl.multiple_of((i % per) * BLK, BLK)
        for j, r_ref in enumerate((r0, r1, r2, r3)):
            @pl.when((t ^ j) == i // per)
            def _():
                r_ref[pl.ds(place, BLK), :] = part
        return carry

    lax.fori_loop(0, NB, block, 0)


def full(shape):
    return pl.BlockSpec(shape, lambda *_: (0,) * len(shape))


def attn_fwd(t, pieces, w, wo, cos, sin, segc, segr):
    out_shape = (
        [jax.ShapeDtypeStruct((ROW, 3 * WL), BF), jax.ShapeDtypeStruct((ROW, WL), BF),
         jax.ShapeDtypeStruct((8, ROW), F32)]
        + [jax.ShapeDtypeStruct((PIECE, D), BF)] * TP
    )
    return pl.pallas_call(
        attn_fwd_body,
        out_shape=out_shape,
        grid_spec=pltpu.PrefetchScalarGridSpec(
            num_scalar_prefetch=1,
            grid=(1,),
            in_specs=[full((PIECE, D))] * TP + [full((D, 3 * WL)), full((WL, D)), full((ROW, 128)),
                      full((ROW, 128)), full((ROW, 1)), full((1, ROW))],
            out_specs=[full(s.shape) for s in out_shape],
        ),
        compiler_params=pltpu.CompilerParams(vmem_limit_bytes=VMEM_LIMIT),
        cost_estimate=pl.CostEstimate(flops=12 * 10**9, bytes_accessed=20 * 10**6, transcendentals=6 * 10**6),
        name="attn_fwd",
    )(t, *pieces, w, wo, cos, sin, segc, segr)


def attn_bwd_body(t_ref, g0, g1, g2, g3, wo_ref, qkv_ref, o_ref, lse_ref, cos_ref, sin_ref, segc_ref, segr_ref,
                  dp_ref, gwo_ref, do_s, dk_s, dv_s, p_s, ds_s, qm_s, dm_s):
    t = t_ref[0]
    low = lax.broadcasted_iota(jnp.int32, (BLK, 128), 1) % HEAD_DIM < HEAD_DIM // 2
    gwo = jnp.zeros((WL, D), F32)
    for j, g_ref in enumerate((g0, g1, g2, g3)):
        row = pl.multiple_of((t ^ j) * PIECE, PIECE)
        do_s[pl.ds(row, PIECE), :] = mm(g_ref[...], wo_ref[...], NT).astype(BF)
        gwo += mm(o_ref[pl.ds(row, PIECE), :], g_ref[...], TN)
    gwo_ref[...] = gwo.astype(BF)
    dk_s[...] = jnp.zeros_like(dk_s)
    dv_s[...] = jnp.zeros_like(dv_s)
    masks = [head_mask(h, BLK, BF) for h in range(HL)]
    feature = lax.broadcasted_iota(jnp.int32, (WL, BLK), 0) // HEAD_DIM

    def unrope(u, row):
        cos = cos_ref[pl.ds(row, BLK), :]
        sin = -sin_ref[pl.ds(row, BLK), :]
        return [rope_slab(u[:, s * 128:(s + 1) * 128], cos, sin, low).astype(BF) for s in range(WL // 128)]

    def block(i, carry):
        row = pl.multiple_of(i * BLK, BLK)
        start = span_start(i)
        q = qkv_ref[pl.ds(row, BLK), :WL]
        g = do_s[pl.ds(row, BLK), :]
        k = qkv_ref[pl.ds(start, SPAN), WL:2 * WL]
        v = qkv_ref[pl.ds(start, SPAN), 2 * WL:]
        bias = jnp.where(segc_ref[pl.ds(start, SPAN), :] == segr_ref[0:1, pl.ds(row, BLK)], 0.0, -1e30)
        for h in range(HL):
            qm = q * masks[h]
            gm = g * masks[h]
            cols = slice(h * BLK, (h + 1) * BLK)
            qm_s[cols, :] = qm
            dm_s[cols, :] = gm
            p = jnp.exp(mm(k, qm, NT) + bias - lse_ref[h:h + 1, pl.ds(row, BLK)])
            dp = mm(v, gm, NT)
            inner = jnp.sum(p * dp, axis=0, keepdims=True)
            p_s[:, cols] = p.astype(BF)
            ds_s[:, cols] = (p * (dp - inner)).astype(BF)
        dv_s[pl.ds(start, SPAN), :] += mm(p_s[...], dm_s[...])
        dk_s[pl.ds(start, SPAN), :] += mm(ds_s[...], qm_s[...])
        wide = mm(k, ds_s[...], TN)
        dq = jnp.zeros((WL, BLK), F32)
        for h in range(HL):
            dq += jnp.where(feature == h, wide[:, h * BLK:(h + 1) * BLK], 0.0)
        dq = (dq * (HEAD_DIM ** -0.5)).T
        for s, piece in enumerate(unrope(dq, row)):
            dp_ref[pl.ds(row, BLK), s * 128:(s + 1) * 128] = piece
        return carry

    lax.fori_loop(0, NB, block, 0)

    def finish(i, carry):
        row = pl.multiple_of(i * BLK, BLK)
        for s, piece in enumerate(unrope(dk_s[pl.ds(row, BLK), :], row)):
            dp_ref[pl.ds(row, BLK), WL + s * 128:WL + (s + 1) * 128] = piece
        dp_ref[pl.ds(row, BLK), 2 * WL:] = dv_s[pl.ds(row, BLK), :].astype(BF)
        return carry

    lax.fori_loop(0, NB, finish, 0)


def attn_bwd(t, pieces, wo, qkv, o, lse, cos, sin, segc, segr):
    out_shape = [jax.ShapeDtypeStruct((ROW, 3 * WL), BF), jax.ShapeDtypeStruct((WL, D), BF)]
    return pl.pallas_call(
        attn_bwd_body,
        out_shape=out_shape,
        grid_spec=pltpu.PrefetchScalarGridSpec(
            num_scalar_prefetch=1,
            grid=(1,),
            in_specs=[full((PIECE, D))] * TP + [full((WL, D)), full((ROW, 3 * WL)), full((ROW, WL)), full((8, ROW)),
                      full((ROW, 128)), full((ROW, 128)), full((ROW, 1)), full((1, ROW))],
            out_specs=[full(s.shape) for s in out_shape],
            scratch_shapes=[pltpu.VMEM((ROW, WL), BF), pltpu.VMEM((ROW, WL), F32), pltpu.VMEM((ROW, WL), F32),
                            pltpu.VMEM((SPAN, HL * BLK), BF), pltpu.VMEM((SPAN, HL * BLK), BF),
                            pltpu.VMEM((HL * BLK, WL), BF), pltpu.VMEM((HL * BLK, WL), BF)],
        ),
        compiler_params=pltpu.CompilerParams(vmem_limit_bytes=VMEM_LIMIT),
        cost_estimate=pl.CostEstimate(flops=20 * 10**9, bytes_accessed=20 * 10**6, transcendentals=6 * 10**6),
        name="attn_bwd",
    )(t, *pieces, wo, qkv, o, lse, cos, sin, segc, segr)


def ffn_body(ax, ay, cx, cy, w_ref, h_ref, dg_ref, dx, dy):
    i = pl.program_id(0)
    first = i < PIECE // BLK
    a = jnp.where(first, ax[...], ay[...])
    c = jnp.where(first, cx[...], cy[...])
    w_in = w_ref[:, :2 * FL]
    gate_up = mm(a, w_in)
    dh = mm(c, w_ref[:, 2 * FL:], NT)
    gate, up = gate_up[:, :FL], gate_up[:, FL:]
    sig = 1.0 / (1.0 + jnp.exp(-gate))
    act = gate * sig
    h_ref[...] = (act * up).astype(BF)
    dg_ref[:, :FL] = (dh * up * (sig * (1.0 + gate * (1.0 - sig)))).astype(BF)
    dg_ref[:, FL:] = (dh * act).astype(BF)
    da = mm(dg_ref[...], w_in, NT).astype(BF)

    @pl.when(first)
    def _():
        dx[...] = da

    @pl.when(jnp.logical_not(first))
    def _():
        dy[...] = da


def ffn(ax, ay, cx, cy, w):
    per = PIECE // BLK
    sx = pl.BlockSpec((BLK, D), lambda i: (jnp.minimum(i, per - 1), 0))
    sy = pl.BlockSpec((BLK, D), lambda i: (jnp.maximum(i - per, 0), 0))
    out_shape = [jax.ShapeDtypeStruct((2 * PIECE, FL), BF), jax.ShapeDtypeStruct((2 * PIECE, 2 * FL), BF),
                 jax.ShapeDtypeStruct((PIECE, D), BF), jax.ShapeDtypeStruct((PIECE, D), BF)]
    return pl.pallas_call(
        ffn_body,
        out_shape=out_shape,
        grid=(2 * per,),
        in_specs=[sx, sy, sx, sy, full((D, 3 * FL))],
        out_specs=[pl.BlockSpec((BLK, FL), lambda i: (i, 0)), pl.BlockSpec((BLK, 2 * FL), lambda i: (i, 0)), sx, sy],
        compiler_params=pltpu.CompilerParams(vmem_limit_bytes=VMEM_LIMIT),
        cost_estimate=pl.CostEstimate(flops=11 * 10**9, bytes_accessed=18 * 10**6, transcendentals=2 * 10**6),
        name="ffn",
    )(ax, ay, cx, cy, w)


def adam_update(weight, first_moment, second_moment, gradient, factor, use_decay, rate):
    clipped = gradient * factor
    first_new = beta_one * first_moment + (1.0 - beta_one) * clipped
    second_new = beta_two * second_moment + (1.0 - beta_two) * clipped * clipped
    first_hat = first_new / (1.0 - beta_one**STEP)
    second_hat = second_new / (1.0 - beta_two**STEP)
    direction = first_hat / (jnp.sqrt(second_hat) + adam_eps) + use_decay * weight_decay * weight
    return (clipped, weight - rate * direction, first_new, second_new)


def per_device(
    tokens, cotangent, lengths,
    qkv_master, qkv_first, qkv_second,
    out_master, out_first, out_second,
    in_master, in_first, in_second,
    down_master, down_first, down_second,
    norm_gains, gain_first, gain_second,
):
    shards = lax.axis_size("dp")
    rows = D // shards
    t = lax.axis_index("tensor").astype(jnp.int32).reshape(1)

    parts = D // WL
    out_low = out_master.astype(BF)
    out_tall = jnp.concatenate([out_low[:, j * WL:(j + 1) * WL] for j in range(parts)], axis=0)
    first = jnp.concatenate([qkv_master.reshape(rows, 3 * WL).astype(BF), out_tall], axis=1)
    second = jnp.concatenate([in_master.reshape(rows, 2 * FL).astype(BF), down_master.astype(BF)], axis=1)
    first = lax.all_gather(first, "dp", axis=0, tiled=True)
    second = lax.all_gather(second, "dp", axis=0, tiled=True)
    w_qkv = first[:, :3 * WL]
    w_out = (first[:, 3 * WL:].reshape(shards, parts, rows // parts, WL)
             .transpose(0, 2, 1, 3).reshape(WL, D))

    ends = jnp.cumsum(lengths[0])
    place_c = lax.broadcasted_iota(jnp.int32, (ROW, 1), 0)
    passed = (place_c >= ends[None, :]).astype(jnp.int32)
    segc = jnp.sum(passed, axis=1, keepdims=True)
    offset = place_c - jnp.sum(passed * lengths[0][None, :], axis=1, keepdims=True)
    place_r = lax.broadcasted_iota(jnp.int32, (1, ROW), 1)
    segr = jnp.sum((place_r >= ends[:, None]).astype(jnp.int32), axis=0, keepdims=True)
    half = HEAD_DIM // 2
    inverse = jnp.exp((jnp.arange(128) % half).astype(F32) * (-2.0 * math.log(10000.0) / HEAD_DIM))
    angles = offset.astype(F32) * inverse[None, :]
    sign = jnp.where(jnp.arange(128) % HEAD_DIM < half, -1.0, 1.0).astype(F32)
    cos, sin = jnp.cos(angles), jnp.sin(angles) * sign[None, :]

    x = tokens.astype(F32)
    a1 = gather_pieces(layer_norm(x, norm_gains[0]).astype(BF))
    cot = gather_pieces(cotangent)
    qkv, o, lse, *parts_r = attn_fwd(t, a1, w_qkv, w_out, cos, sin, segc, segr)
    middle = x + scatter_sum(*parts_r)
    a2 = gather_pieces(layer_norm(middle, norm_gains[1]).astype(BF))
    h_near, dg_near, d0, d1 = ffn(a2[0], a2[1], cot[0], cot[1], second)
    h_far, dg_far, d2, d3 = ffn(a2[2], a2[3], cot[2], cot[3], second)
    da2 = scatter_sum(d0, d1, d2, d3)

    a2_all = jnp.concatenate(a2, axis=0)
    cot_all = jnp.concatenate(cot, axis=0)
    h_all = jnp.concatenate([h_near, h_far], axis=0)
    dg_all = jnp.concatenate([dg_near, dg_far], axis=0)
    grad_down = mm(h_all, cot_all, TN).astype(BF)
    grad_in = mm(a2_all, dg_all, TN).astype(BF)
    w_down = second[:, 2 * FL:]
    outs = [mm(h[s * PIECE:(s + 1) * PIECE], w_down).astype(BF) for h in (h_near, h_far) for s in range(2)]
    layer_out = (middle + scatter_sum(*outs)).astype(BF)

    back, gain_two_grad = jax.vjp(layer_norm, middle, norm_gains[1])[1](da2)
    middle_grad = cotangent.astype(F32) + back
    g = gather_pieces(middle_grad.astype(BF))
    d_qkv, grad_out = attn_bwd(t, g, w_out, qkv, o, lse, cos, sin, segc, segr)

    a1_all = jnp.stack(a1)
    order = t[0] ^ jnp.arange(TP, dtype=jnp.int32)
    a1_row = jnp.concatenate([lax.dynamic_index_in_dim(a1_all, order[j], 0, keepdims=False) for j in range(TP)], axis=0)
    grad_qkv = mm(a1_row, d_qkv, TN).astype(BF)
    d_pieces = d_qkv.reshape(TP, PIECE, 3 * WL)
    back1 = [mm(lax.dynamic_index_in_dim(d_pieces, order[j], 0, keepdims=False), w_qkv, NT).astype(BF) for j in range(TP)]
    input_back, gain_one_grad = jax.vjp(layer_norm, x, norm_gains[0])[1](scatter_sum(*back1))
    input_grad = middle_grad + input_back

    out_tall = (grad_out.reshape(shards, rows // parts, parts, WL).transpose(0, 2, 1, 3).reshape(D, WL))
    scatter = functools.partial(lax.psum_scatter, axis_name="dp", scatter_dimension=0, tiled=True)
    red_down = scatter(grad_down).astype(F32)
    red_in = scatter(grad_in).astype(F32)
    red_first = scatter(jnp.concatenate([grad_qkv, out_tall], axis=1)).astype(F32)
    red_qkv = red_first[:, :3 * WL]
    red_out = jnp.concatenate(
        [red_first[j * (rows // parts):(j + 1) * (rows // parts), 3 * WL:] for j in range(parts)], axis=1)

    squares = (jnp.sum(red_first * red_first) + jnp.sum(red_in * red_in) + jnp.sum(red_down * red_down))
    total = jnp.stack([gain_one_grad, gain_two_grad, jnp.full((D,), squares)])
    for axis in ("tensor", "dp"):
        k = 1
        while k < lax.axis_size(axis):
            total = total + swap(total, axis, k)
            k *= 2
    gain_total = total[:2]
    grad_norm = jnp.sqrt(total[2, 0] + jnp.sum(gain_total * gain_total))
    factor = max_norm / jnp.maximum(grad_norm, max_norm)
    qkv_res = adam_update(qkv_master, qkv_first, qkv_second, red_qkv.reshape(qkv_master.shape), factor, 1.0, learn_rate)
    out_res = adam_update(out_master, out_first, out_second, red_out, factor, 1.0, learn_rate)
    in_res = adam_update(in_master, in_first, in_second, red_in.reshape(in_master.shape), factor, 1.0, learn_rate)
    down_res = adam_update(down_master, down_first, down_second, red_down, factor, 1.0, learn_rate)
    gain_res = adam_update(norm_gains, gain_first, gain_second, gain_total, factor, 0.0, gain_rate)
    return (layer_out, input_grad, *qkv_res, *out_res, *in_res, *down_res, *gain_res, grad_norm)


def solution(mesh):
    token = P(("dp", "tensor"), None)
    wide = P("dp", None, "tensor")
    tall = P(("tensor", "dp"), None)
    placed = (token, token, P("dp", None)) + (wide,) * 3 + (tall,) * 3 + (wide,) * 3 + (tall,) * 3 + (P(),) * 3
    out_specs = (token, token) + (wide,) * 4 + (tall,) * 4 + (wide,) * 4 + (tall,) * 4 + (P(),) * 5
    return jax.shard_map(per_device, mesh=mesh, in_specs=placed, out_specs=out_specs, check_vma=False)
```
